128 devices in a mesh: layer: 16 (over y_hi, z, core), feat: 2 (over y_lo), tok: 4 (over x).
Axes of the slice: x: 4, y: 4 (y_hi: 2, y_lo: 2; y = y_hi * 2 + y_lo), z: 4, core: 2. Of those that a mesh axis runs over, the one named last changes fastest.
Arguments:
- sublevel_entries: bfloat16 [16, 1024, 1152], P('layer', 'tok'), may hold values from -6 to 6
- readin_matrix: bfloat16 [16, 1152, 8192], P('layer', None, ('feat', 'tok')), may hold values from -0.1875 to 0.1875
- readin_offset: float32 [16, 8192], P('layer', ('feat', 'tok')), may hold values from -3 to 3
- cutoff_exceeded: int32 [16, 1024, 8192], P('layer', None, ('feat', 'tok')), may hold values 0 or 1
- writeout_matrix: bfloat16 [16, 2, 8192, 1152], P('layer', None, ('feat', 'tok')), may hold values from -0.0625 to 0.0625
- hidden_block_result: bfloat16 [2, 1024, 1152], P(None, 'tok'), may hold values from -6 to 6
- writing_depth_number: int32 [2], replicated, may hold values from 0 to 15, as said below
Outputs:
- enc_grad: bfloat16 [16, 1152, 8192], P('layer', None, ('feat', 'tok'))
- dec_grad: bfloat16 [16, 2, 8192, 1152], P('layer', None, ('feat', 'tok'))
- bias_grad: float32 [16, 8192], P('layer', ('feat', 'tok'))
The draws below stay inside these ranges and needn't reach their ends.
Inputs may be any that keep to these rules, and one draw needn't show every extreme that they name: `writing_depth_number`: one of the two entries is 15 and the other is smaller; either may come first.
All inputs are finite; a program needn't handle non-finite values. No bound on the sum of `cutoff_exceeded` on one device may be relied on, other than what follows from the above.
Results may differ from the reference program's by a relative error of at most 0.007.
Values may be sent and summed in bfloat16 or wider, within the bound.
A program may use at most 128 MiB of HBM per device.

```python
import math
import jax
import jax.numpy as jnp
from jax import lax

D = 1152
LATENT_WIDTH = 8192
TARGETS = 2
READ_DEPTHS = 16
POSITION_NUMBER = 1024


def draw_writing_depth_number(key, part):
    shallow = jax.random.randint(jax.random.fold_in(key, 4093), (1,), 0, READ_DEPTHS - 1).astype(jnp.int32)
    deepest = jnp.full((1,), READ_DEPTHS - 1, jnp.int32)
    flipped = jax.random.randint(jax.random.fold_in(key, 7919), (1,), 0, 2).astype(jnp.int32)
    first = flipped * deepest + (1 - flipped) * shallow
    second = flipped * shallow + (1 - flipped) * deepest
    return jnp.concatenate([first, second]).astype(jnp.int32)


def set_ends(values, rng, least, largest):
    longest = values.shape.index(max(values.shape))
    spots = []
    for shift in (0, 1):
        where = [jax.random.randint(jax.random.fold_in(rng, axis), (), 0, length) for axis, length in enumerate(values.shape)]
        where[longest] = (where[longest] + shift) % values.shape[longest]
        spots.append(tuple(where))
    return values.at[spots[0]].set(least).at[spots[1]].set(largest)


def steps_of(key, extent, split, low, largest):
    def one(position, shards_of):
        heights = jax.random.uniform(jax.random.fold_in(jax.random.fold_in(key, 6), position), (shards_of,), jnp.float32, low / len(split), largest / len(split))
        return jnp.repeat(jnp.exp(heights), extent[position] // shards_of).reshape((-1,) + (1,) * (len(extent) - position - 1))

    level = one(*split[0])
    for cut in split[1:]:
        level = level * one(*cut)
    return level


def noise(key, dims, deviation, most, split=(), held_as=jnp.bfloat16):
    result = deviation * jax.random.normal(key, dims, jnp.float32)
    if split:
        result = result * steps_of(key, dims, split, -0.22, 0.18)
    return jnp.clip(result, -most, most).astype(held_as)


def setup_inputs(seed: int = 0) -> dict:
    key_of = jax.random.split(jax.random.key(seed), 8)
    sublevel_entries = noise(key_of[0], (READ_DEPTHS, POSITION_NUMBER, D), 1.0, 6.0, ((0, 16), (1, 4)))
    readin_matrix = noise(key_of[1], (READ_DEPTHS, D, LATENT_WIDTH), D ** -0.5, 0.1875, ((0, 16), (2, 8)))
    readin_offset = noise(key_of[2], (READ_DEPTHS, LATENT_WIDTH), 0.5, 3.0, ((0, 16), (1, 8)), jnp.float32)
    cutoff_exceeded = set_ends((jax.random.randint(key_of[3], (READ_DEPTHS, POSITION_NUMBER, LATENT_WIDTH), 0, 4) < 1).astype(jnp.int32), jax.random.fold_in(key_of[3], 1), 0, 1)
    writeout_matrix = noise(key_of[4], (READ_DEPTHS, TARGETS, LATENT_WIDTH, D), LATENT_WIDTH ** -0.5, 0.0625, ((0, 16), (2, 8)))
    hidden_block_result = noise(key_of[5], (TARGETS, POSITION_NUMBER, D), 1.0, 6.0, ((1, 4),))
    writing_depth_number = draw_writing_depth_number(jax.random.fold_in(key_of[7], 71), 0)
    return {"sublevel_entries": sublevel_entries, "readin_matrix": readin_matrix, "readin_offset": readin_offset, "cutoff_exceeded": cutoff_exceeded, "writeout_matrix": writeout_matrix, "hidden_block_result": hidden_block_result, "writing_depth_number": writing_depth_number}


def reference(sublevel_entries, readin_matrix, readin_offset, cutoff_exceeded, writeout_matrix, hidden_block_result, writing_depth_number):
    inverse = 1.0 / math.sqrt(POSITION_NUMBER)
    rebuilt = -hidden_block_result.astype(jnp.float32)
    acts_list = []
    for reading_depth in range(READ_DEPTHS):
        encoded_prejump_signal = jnp.dot(sublevel_entries[reading_depth], readin_matrix[reading_depth], preferred_element_type=jnp.float32) + readin_offset[reading_depth][None, :]
        sparse_code_entries = (encoded_prejump_signal * cutoff_exceeded[reading_depth].astype(jnp.float32)).astype(jnp.bfloat16)
        acts_list.append(sparse_code_entries)
        live_mask = (reading_depth <= writing_depth_number).astype(jnp.float32)
        for desired_reconstruction in range(TARGETS):
            rebuilt = rebuilt.at[desired_reconstruction].add(live_mask[desired_reconstruction] * jnp.dot(sparse_code_entries, writeout_matrix[reading_depth, desired_reconstruction], preferred_element_type=jnp.float32))
    scaled = (rebuilt * inverse).astype(jnp.bfloat16)
    enc_list = []
    dec_list = []
    bias_list = []
    for reading_depth in range(READ_DEPTHS):
        sparse_code_entries = acts_list[reading_depth]
        live_mask = (reading_depth <= writing_depth_number).astype(jnp.float32)
        dec_rows = []
        code_sensitivity = jnp.zeros((POSITION_NUMBER, LATENT_WIDTH), jnp.float32)
        for desired_reconstruction in range(TARGETS):
            dec_rows.append((jnp.dot(sparse_code_entries.T, scaled[desired_reconstruction], preferred_element_type=jnp.float32) * live_mask[desired_reconstruction]).astype(jnp.bfloat16))
            code_sensitivity = code_sensitivity + live_mask[desired_reconstruction] * jnp.dot(scaled[desired_reconstruction], writeout_matrix[reading_depth, desired_reconstruction].T, preferred_element_type=jnp.float32)
        prejump_sensitivity = code_sensitivity * cutoff_exceeded[reading_depth].astype(jnp.float32)
        bias_list.append(lax.optimization_barrier(jnp.sum(prejump_sensitivity, axis=0)))
        enc_list.append(jnp.dot(sublevel_entries[reading_depth].T, prejump_sensitivity.astype(jnp.bfloat16), preferred_element_type=jnp.float32).astype(jnp.bfloat16))
        dec_list.append(jnp.stack(dec_rows))
    return (jnp.stack(enc_list), jnp.stack(dec_list), jnp.stack(bias_list))
```

```python
import functools
import math

import jax
import jax.numpy as jnp
from jax import lax
from jax.experimental import pallas as pl
from jax.experimental.pallas import tpu as pltpu
from jax.sharding import PartitionSpec as P

MESH = pl.DeviceIdType.MESH
F32, BF16 = jnp.float32, jnp.bfloat16
ROUNDS = 4
NT = (((1,), (1,)), ((), ()))
TN = (((0,), (0,)), ((), ()))
GAP = {"F": 0.0, "E": 4.8, "1": 9.3, "2": 15.1, "3": 17.8, "4": 20.6, "5": 23.1, "6": 28.6, "7": 31.1}
PERIOD = 4.9


def sent(R):
    slots = {}
    for name, count in (("g", 4), ("p", 1), ("a1", 3), ("b1", 3), ("a2", 3), ("b2", 3), ("x", 3),
                        ("ga1", 3), ("gb1", 3), ("ga2", 3), ("gb2", 3), ("fa", 1), ("fb", 1)):
        for i in range(count):
            slots[name, i] = len(slots)
    return slots


def comm_kernel(cfg, live_ref, x_hbm, wr_hbm, off_ref, gate_hbm, wo_hbm, hid_hbm,
                bias_ref, g_out, acts_out, low_out, sa_out, sb_out,
                g, wr, gate, wo, hid, acts, low, pk, cs, cr, s1a, s1b, r1a, r1b, k2a, k2b, s2a, s2b, r2a, r2b,
                k3, s3, r3, sa, sb, send_sem, recv_sem, in_sem, own_sem, out_sem):
    R, TB, D, DA, Fw, inverse = cfg
    DB = D - DA
    M, PR, HB = 4 * TB, TB // 4, TB // 2
    slots = sent(R)
    layer, feat, x = lax.axis_index("layer"), lax.axis_index("feat"), lax.axis_index("tok")
    c = lax.rem(layer, 2)
    z = lax.rem(lax.div(layer, 2), 4)
    y = lax.div(layer, 8) * 2 + feat
    other = 1 - c

    def xpeer(o):
        return (layer, feat, lax.rem(x + o, 4))

    def zpeer(o):
        return (lax.div(layer, 8) * 8 + lax.rem(z + o, 4) * 2 + c, feat, x)

    def ypeer(o):
        yy = lax.rem(y + o, 4)
        return (lax.div(yy, 2) * 8 + z * 2 + c, lax.rem(yy, 2), x)

    partner = (lax.div(layer, 2) * 2 + other, feat, x)

    def at(index, size):
        return pl.ds(pl.multiple_of(index * size, size), size)

    def remote(j, name, i, src, dst, device):
        k = slots[name, i]
        return pltpu.make_async_remote_copy(
            src_ref=src, dst_ref=dst, send_sem=send_sem.at[j, k], recv_sem=recv_sem.at[j, k],
            device_id=device, device_id_type=MESH)

    started = []

    def send(j, name, i, src, dst, device):
        copy = remote(j, name, i, src, dst, device)
        copy.start()
        started.append(copy)

    def arrive(j, name, i, dst):
        remote(j, name, i, dst, dst, partner).wait_recv()

    loads = [pltpu.make_async_copy(a, b, in_sem.at[i]) for i, (a, b) in enumerate(
        ((wr_hbm, wr), (gate_hbm, gate), (wo_hbm, wo), (hid_hbm, hid)))]
    own = [pltpu.make_async_copy(x_hbm.at[pl.ds(j * TB, TB)], g.at[j, at(x, TB)], own_sem.at[j]) for j in range(R)]
    for j in range(R):
        own[j].start()
    for copy in loads:
        copy.start()
    bias_ref[...] = jnp.zeros_like(bias_ref)

    barrier = pltpu.get_barrier_semaphore()
    peers = [p(o) for p in (xpeer, ypeer, zpeer) for o in (1, 3, 2)] + [partner]
    for p in peers:
        pl.semaphore_signal(barrier, inc=1, device_id=p, device_id_type=MESH)
    pl.semaphore_wait(barrier, len(peers))

    def gather_own(j):
        src = x_hbm.at[pl.ds(j * TB, TB)]
        send(j, "g", 0, src, g.at[j, at(x, TB)], xpeer(1))
        send(j, "g", 1, src, g.at[j, at(x, TB)], xpeer(3))

    outs = []

    def put(src, dst):
        copy = pltpu.make_async_copy(src, dst, out_sem.at[len(outs)])
        copy.start()
        outs.append(copy)

    def stage_f(j):
        left, right = lax.rem(x + 3, 4), lax.rem(x + 1, 4)
        arrive(j, "g", 0, g.at[j, at(left, TB)])
        rows = pl.ds(pl.multiple_of(left * TB, TB), HB)
        send(j, "g", 2, g.at[j, rows], g.at[j, rows], xpeer(1))
        arrive(j, "g", 1, g.at[j, at(right, TB)])
        rows = pl.ds(pl.multiple_of(right * TB + HB, HB), HB)
        send(j, "g", 3, g.at[j, rows], g.at[j, rows], xpeer(3))
        if j + 2 < R:
            gather_own(j + 2)

    def stage_e(j):
        far = lax.rem(x + 2, 4)
        arrive(j, "g", 2, g.at[j, pl.ds(pl.multiple_of(far * TB, TB), HB)])
        arrive(j, "g", 3, g.at[j, pl.ds(pl.multiple_of(far * TB + HB, HB), HB)])
        own[j].wait()
        put(g.at[j], g_out.at[j])
        if j == 0:
            loads[0].wait()
            loads[1].wait()

        @pl.loop(0, Fw // 256)
        def _(n):
            cols = pl.ds(pl.multiple_of(n * 256, 256), 256)
            pre = jnp.dot(g[j], wr[:, cols], preferred_element_type=F32) + off_ref[:, cols]
            for t in range(4):
                rows = slice(t * TB, (t + 1) * TB)
                acts[j, rows, cols] = (pre[rows] * gate[t, j * TB:(j + 1) * TB, cols].astype(F32)).astype(BF16)

        if j == 0:
            loads[2].wait()

        @pl.loop(0, D // 384)
        def _(n):
            cols = pl.ds(pl.multiple_of(n * 384, 128), 384)
            part = jnp.dot(acts[j], wo[other, :, cols], preferred_element_type=F32)
            cs[j, :, cols] = (part * live_ref[other]).astype(BF16)

        send(j, "p", 0, cs.at[j], cr.at[j], partner)
        put(acts.at[j], acts_out.at[j])

        @pl.loop(0, D // 384)
        def _(n):
            cols = pl.ds(pl.multiple_of(n * 384, 128), 384)
            part = jnp.dot(acts[j], wo[c, :, cols], preferred_element_type=F32)
            pk[j, :, cols] = part * live_ref[c]

    def stage_1(j):
        arrive(j, "p", 0, cr.at[j])
        s1a[j] = (pk[j, :, :DA] + cr[j, :, :DA].astype(F32)).astype(BF16)
        for o in (2, 1, 3):
            send(j, "a1", o - 1, s1a.at[j, at(lax.rem(z + o, 4), TB)], r1a.at[j, o - 1], zpeer(o))
        s1b[j] = (pk[j, :, DA:] + cr[j, :, DA:].astype(F32)).astype(BF16)
        for o in (2, 1, 3):
            send(j, "b1", o - 1, s1b.at[j, at(lax.rem(y + o, 4), TB)], r1b.at[j, o - 1], ypeer(o))

    def stage_2(j):
        for name, r1, q, k2, s2, r2, lanes, p, me, out in (
                ("a1", r1a, z, k2a, s2a, r2a, slice(0, DA), ypeer, y, "a2"),
                ("b1", r1b, y, k2b, s2b, r2b, slice(DA, D), zpeer, z, "b2")):
            total = pk[j, at(q, TB), lanes] + cr[j, at(q, TB), lanes].astype(F32)
            for i in (0, 2, 1):
                arrive(j, name, i, r1.at[j, i])
                total = total + r1[j, i].astype(F32)
            k2[j] = total
            s2[j] = total.astype(BF16)
            for o in (2, 1, 3):
                send(j, out, o - 1, s2.at[j, at(lax.rem(me + o, 4), PR)], r2.at[j, o - 1], p(o))

    def stage_3(j):
        if j == 0:
            loads[3].wait()
        for name, r2, me, k2, lanes, q in (("a2", r2a, y, k2a, slice(0, DA), z), ("b2", r2b, z, k2b, slice(DA, D), y)):
            total = k2[j, at(me, PR)]
            for i in (0, 2, 1):
                arrive(j, name, i, r2.at[j, i])
                total = total + r2[j, i].astype(F32)
            owner = (q == x).astype(F32)
            total = total - owner * hid[c, pl.ds(pl.multiple_of(j * TB + me * PR, PR), PR), lanes].astype(F32)
            k3[j, :, lanes] = total
            s3[j, :, lanes] = total.astype(BF16)
        for o in (2, 1, 3):
            send(j, "x", o - 1, s3.at[j], r3.at[j, o - 1], xpeer(o))

    def stage_4(j):
        total = k3[j]
        for i in (0, 2, 1):
            arrive(j, "x", i, r3.at[j, i])
            total = total + r3[j, i].astype(F32)
        scaled = (total * inverse).astype(BF16)
        arows = pl.ds(pl.multiple_of(z * TB + y * PR, PR), PR)
        brows = pl.ds(pl.multiple_of(y * TB + z * PR, PR), PR)
        sa[c, j, arows] = scaled[:, :DA]
        sb[c, j, brows] = scaled[:, DA:]
        for o in (2, 1, 3):
            send(j, "ga1", o - 1, sa.at[c, j, arows], sa.at[c, j, arows], ypeer(o))
            send(j, "gb1", o - 1, sb.at[c, j, brows], sb.at[c, j, brows], zpeer(o))

    def stage_5(j):
        for i, o in ((0, 3), (2, 1), (1, 2)):
            yy, zz = lax.rem(y + o, 4), lax.rem(z + o, 4)
            arrive(j, "ga1", i, sa.at[c, j, pl.ds(pl.multiple_of(z * TB + yy * PR, PR), PR)])
            arrive(j, "gb1", i, sb.at[c, j, pl.ds(pl.multiple_of(y * TB + zz * PR, PR), PR)])
        for o in (2, 1, 3):
            send(j, "ga2", o - 1, sa.at[c, j, at(z, TB)], sa.at[c, j, at(z, TB)], zpeer(o))
            send(j, "gb2", o - 1, sb.at[c, j, at(y, TB)], sb.at[c, j, at(y, TB)], ypeer(o))

    def stage_6(j):
        for i, o in ((0, 3), (2, 1), (1, 2)):
            yy, zz = lax.rem(y + o, 4), lax.rem(z + o, 4)
            arrive(j, "ga2", i, sa.at[c, j, at(zz, TB)])
            arrive(j, "gb2", i, sb.at[c, j, at(yy, TB)])
        send(j, "fa", 0, sa.at[c, j], sa.at[c, j], partner)
        send(j, "fb", 0, sb.at[c, j], sb.at[c, j], partner)
        put(sa.at[c, j], sa_out.at[c, j])
        put(sb.at[c, j], sb_out.at[c, j])

    def stage_7(j):
        arrive(j, "fa", 0, sa.at[other, j])
        arrive(j, "fb", 0, sb.at[other, j])
        put(sa.at[other, j], sa_out.at[other, j])
        put(sb.at[other, j], sb_out.at[other, j])

        @pl.loop(0, Fw // 256)
        def _(n):
            cols = pl.ds(pl.multiple_of(n * 256, 256), 256)
            total = jnp.zeros((M, 256), F32)
            for t in range(2):
                part = lax.dot_general(sa[t, j], wo[t, cols, :DA], NT, preferred_element_type=F32)
                part = part + lax.dot_general(sb[t, j], wo[t, cols, DA:], NT, preferred_element_type=F32)
                total = total + live_ref[t] * part
            for t in range(4):
                rows = slice(t * TB, (t + 1) * TB)
                pre = total[rows] * gate[t, j * TB:(j + 1) * TB, cols].astype(F32)
                bias_ref[:, cols] += jnp.sum(pre, axis=0, keepdims=True)
                low[j, rows, cols] = pre.astype(BF16)

        put(low.at[j], low_out.at[j])

    gather_own(0)
    if R > 1:
        gather_own(1)
    stages = {"F": stage_f, "E": stage_e, "1": stage_1, "2": stage_2, "3": stage_3, "4": stage_4, "5": stage_5,
              "6": stage_6, "7": stage_7}
    order = sorted(((PERIOD * j + gap, s, j) for s, gap in GAP.items() for j in range(R)))
    for _, s, j in order:
        stages[s](j)
    for copy in started:
        copy.wait_send()
    for copy in outs:
        copy.wait()


def dec_kernel(live_ref, acts_ref, sa_ref, sb_ref, out_ref):
    DA = sa_ref.shape[-1]
    for t in range(2):
        for ref, lanes in ((sa_ref, slice(0, DA)), (sb_ref, slice(DA, out_ref.shape[-1]))):
            got = lax.dot_general(acts_ref[...], ref[t], TN, preferred_element_type=F32)
            out_ref[t, :, lanes] = (got * live_ref[t]).astype(BF16)


def enc_kernel(x_ref, low_ref, out_ref):
    out_ref[...] = lax.dot_general(x_ref[...], low_ref[...], TN, preferred_element_type=F32).astype(BF16)


def step(entries, readin, offset, cutoff, writeout, hidden, depths):
    R = ROUNDS
    tokens, D = entries.shape[1] * 4, entries.shape[2]
    Fw = readin.shape[2]
    TB = tokens // 4 // R
    M, PR, DA = 4 * TB, TB // 4, 640
    DB = D - DA
    live = (lax.axis_index("layer") <= depths).astype(F32)
    cfg = (R, TB, D, DA, Fw, 1.0 / math.sqrt(tokens))
    n_slots = len(sent(R))
    hbm = pl.BlockSpec(memory_space=pl.ANY)
    vmem = pl.BlockSpec(memory_space=pltpu.VMEM)
    smem = pl.BlockSpec(memory_space=pltpu.SMEM)
    V = pltpu.VMEM
    bias, g, acts, low, sa, sb = pl.pallas_call(
        functools.partial(comm_kernel, cfg),
        out_shape=(
            jax.ShapeDtypeStruct((1, Fw), F32),
            jax.ShapeDtypeStruct((R, M, D), BF16),
            jax.ShapeDtypeStruct((R, M, Fw), BF16),
            jax.ShapeDtypeStruct((R, M, Fw), BF16),
            jax.ShapeDtypeStruct((2, R, M, DA), BF16),
            jax.ShapeDtypeStruct((2, R, M, DB), BF16),
        ),
        in_specs=[smem, hbm, hbm, vmem, hbm, hbm, hbm],
        out_specs=(vmem, hbm, hbm, hbm, hbm, hbm),
        scratch_shapes=[
            V((R, M, D), BF16), V((D, Fw), BF16), V((4, tokens // 4, Fw), jnp.int32), V((2, Fw, D), BF16),
            V((2, tokens // 4, D), BF16), V((R, M, Fw), BF16), V((R, M, Fw), BF16),
            V((R, M, D), F32), V((R, M, D), BF16), V((R, M, D), BF16),
            V((R, M, DA), BF16), V((R, M, DB), BF16), V((R, 3, TB, DA), BF16), V((R, 3, TB, DB), BF16),
            V((R, TB, DA), F32), V((R, TB, DB), F32), V((R, TB, DA), BF16), V((R, TB, DB), BF16),
            V((R, 3, PR, DA), BF16), V((R, 3, PR, DB), BF16),
            V((R, PR, D), F32), V((R, PR, D), BF16), V((R, 3, PR, D), BF16),
            V((2, R, M, DA), BF16), V((2, R, M, DB), BF16),
            pltpu.SemaphoreType.DMA((R, n_slots)), pltpu.SemaphoreType.DMA((R, n_slots)),
            pltpu.SemaphoreType.DMA((4,)), pltpu.SemaphoreType.DMA((R,)), pltpu.SemaphoreType.DMA((7 * R,)),
        ],
        compiler_params=pltpu.CompilerParams(collective_id=0, has_side_effects=True, vmem_limit_bytes=60 * 2**20),
    )(live, entries[0], readin[0], offset, cutoff.reshape(4, tokens // 4, Fw), writeout[0], hidden)

    acts2, low2, g2 = acts.reshape(tokens, Fw), low.reshape(tokens, Fw), g.reshape(tokens, D)
    sa2, sb2 = sa.reshape(2, tokens, DA), sb.reshape(2, tokens, DB)
    dec = pl.pallas_call(
        dec_kernel,
        grid=(Fw // 256,),
        out_shape=jax.ShapeDtypeStruct((2, Fw, D), BF16),
        in_specs=[smem, pl.BlockSpec((tokens, 256), lambda i: (0, i)),
                  pl.BlockSpec((2, tokens, DA), lambda i: (0, 0, 0)), pl.BlockSpec((2, tokens, DB), lambda i: (0, 0, 0))],
        out_specs=pl.BlockSpec((2, 256, D), lambda i: (0, i, 0)),
        cost_estimate=pl.CostEstimate(flops=4 * tokens * Fw * D, bytes_accessed=12 * 2**20, transcendentals=0),
    )(live, acts2, sa2, sb2)
    enc = pl.pallas_call(
        enc_kernel,
        grid=(D // 384,),
        out_shape=jax.ShapeDtypeStruct((D, Fw), BF16),
        in_specs=[pl.BlockSpec((tokens, 384), lambda i: (0, i)), pl.BlockSpec((tokens, Fw), lambda i: (0, 0))],
        out_specs=pl.BlockSpec((384, Fw), lambda i: (i, 0)),
        cost_estimate=pl.CostEstimate(flops=2 * tokens * Fw * D, bytes_accessed=7 * 2**20, transcendentals=0),
    )(g2, low2)
    return enc[None], dec[None], bias


def solution(mesh):
    return jax.shard_map(
        step,
        mesh=mesh,
        in_specs=(
            P("layer", "tok", None),
            P("layer", None, ("feat", "tok")),
            P("layer", ("feat", "tok")),
            P("layer", None, ("feat", "tok")),
            P("layer", None, ("feat", "tok"), None),
            P(None, "tok", None),
            P(),
        ),
        out_specs=(
            P("layer", None, ("feat", "tok")),
            P("layer", None, ("feat", "tok"), None),
            P("layer", ("feat", "tok")),
        ),
        check_vma=False,
    )
```

```python
import functools
import math

import jax
import jax.numpy as jnp
from jax import lax
from jax.experimental import pallas as pl
from jax.experimental.pallas import tpu as pltpu
from jax.sharding import PartitionSpec as P

MESH = pl.DeviceIdType.MESH
F32, BF16 = jnp.float32, jnp.bfloat16
ROUNDS = 4
NT = (((1,), (1,)), ((), ()))
TN = (((0,), (0,)), ((), ()))
ORDER = (
    "F0", "F1", "E0", "F2", "10", "E1", "F3", "11", "E2", "20", "E3", "12", "21", "13", "30", "40", "22", "31",
    "23", "50", "32", "41", "33", "42", "60", "51", "70", "43", "52", "61", "53", "71", "62", "72", "63", "73",
)


def sent(R):
    slots = {}
    for name, count in (("g", 4), ("p", 1), ("a1", 3), ("b1", 3), ("a2", 3), ("b2", 3), ("x", 3),
                        ("ga1", 3), ("gb1", 3), ("ga2", 3), ("gb2", 3), ("fa", 1), ("fb", 1)):
        for i in range(count):
            slots[name, i] = len(slots)
    return slots


def comm_kernel(cfg, depth_ref, x_hbm, wr_hbm, off_ref, gate_hbm, wo_hbm, hid_hbm,
                bias_ref, g, acts, low, sa, sb,
                wr, gate, wo, hid, pk, cs, cr, s1a, s1b, r1a, r1b, k2a, k2b, s2a, s2b, r2a, r2b,
                k3, s3, r3, send_sem, recv_sem, in_sem, own_sem):
    R, TB, D, DA, Fw, inverse = cfg
    DB = D - DA
    M, PR, HB = 4 * TB, TB // 4, TB // 2
    slots = sent(R)
    layer, feat, x = lax.axis_index("layer"), lax.axis_index("feat"), lax.axis_index("tok")
    c = lax.rem(layer, 2)
    z = lax.rem(lax.div(layer, 2), 4)
    y = lax.div(layer, 8) * 2 + feat
    other = 1 - c

    def live_of(t):
        return (layer <= depth_ref[t]).astype(F32)

    def xpeer(o):
        return (layer, feat, lax.rem(x + o, 4))

    def zpeer(o):
        return (lax.div(layer, 8) * 8 + lax.rem(z + o, 4) * 2 + c, feat, x)

    def ypeer(o):
        yy = lax.rem(y + o, 4)
        return (lax.div(yy, 2) * 8 + z * 2 + c, lax.rem(yy, 2), x)

    def axes(j):
        pairs = ((zpeer, z), (ypeer, y))
        return pairs if j % 2 == 0 else pairs[::-1]

    partner = (lax.div(layer, 2) * 2 + other, feat, x)

    def at(index, size):
        return pl.ds(pl.multiple_of(index * size, size), size)

    def remote(j, name, i, src, dst, device):
        k = slots[name, i]
        return pltpu.make_async_remote_copy(
            src_ref=src, dst_ref=dst, send_sem=send_sem.at[j, k], recv_sem=recv_sem.at[j, k],
            device_id=device, device_id_type=MESH)

    started = []

    def send(j, name, i, src, dst, device):
        copy = remote(j, name, i, src, dst, device)
        copy.start()
        started.append(copy)

    def arrive(j, name, i, dst):
        remote(j, name, i, dst, dst, partner).wait_recv()

    loads = [pltpu.make_async_copy(a, b, in_sem.at[i]) for i, (a, b) in enumerate(
        ((wr_hbm, wr), (gate_hbm, gate), (wo_hbm, wo), (hid_hbm, hid)))]
    own = [pltpu.make_async_copy(x_hbm.at[pl.ds(j * TB, TB)], g.at[j, at(x, TB)], own_sem.at[j]) for j in range(R)]
    for j in range(R):
        own[j].start()
    for copy in loads:
        copy.start()
    bias_ref[...] = jnp.zeros_like(bias_ref)

    barrier = pltpu.get_barrier_semaphore()
    peers = [p(o) for p in (xpeer, ypeer, zpeer) for o in (1, 3, 2)] + [partner]
    for p in peers:
        pl.semaphore_signal(barrier, inc=1, device_id=p, device_id_type=MESH)
    pl.semaphore_wait(barrier, len(peers))

    def gather_own(j):
        src = x_hbm.at[pl.ds(j * TB, TB)]
        send(j, "g", 0, src, g.at[j, at(x, TB)], xpeer(1))
        send(j, "g", 1, src, g.at[j, at(x, TB)], xpeer(3))

    def stage_f(j):
        left, right = lax.rem(x + 3, 4), lax.rem(x + 1, 4)
        arrive(j, "g", 0, g.at[j, at(left, TB)])
        rows = pl.ds(pl.multiple_of(left * TB, TB), HB)
        send(j, "g", 2, g.at[j, rows], g.at[j, rows], xpeer(1))
        arrive(j, "g", 1, g.at[j, at(right, TB)])
        rows = pl.ds(pl.multiple_of(right * TB + HB, HB), HB)
        send(j, "g", 3, g.at[j, rows], g.at[j, rows], xpeer(3))
        if j + 2 < R:
            gather_own(j + 2)

    def stage_e(j):
        far = lax.rem(x + 2, 4)
        arrive(j, "g", 2, g.at[j, pl.ds(pl.multiple_of(far * TB, TB), HB)])
        arrive(j, "g", 3, g.at[j, pl.ds(pl.multiple_of(far * TB + HB, HB), HB)])
        own[j].wait()
        if j == 0:
            loads[0].wait()
            loads[1].wait()

        pre = jnp.dot(g[j], wr[...], preferred_element_type=F32) + off_ref[...]
        for t in range(4):
            rows = slice(t * TB, (t + 1) * TB)
            acts[j, rows] = (pre[rows] * gate[t, j * TB:(j + 1) * TB].astype(F32)).astype(BF16)
        if j == 0:
            loads[2].wait()
        part = jnp.dot(acts[j], wo[other], preferred_element_type=F32)
        cs[j] = (part * live_of(other)).astype(BF16)
        send(j, "p", 0, cs.at[j], cr.at[j], partner)
        pk[j] = jnp.dot(acts[j], wo[c], preferred_element_type=F32) * live_of(c)

    def stage_1(j):
        arrive(j, "p", 0, cr.at[j])
        (pa, qa), (pb, qb) = axes(j)
        s1a[j] = (pk[j, :, :DA] + cr[j, :, :DA].astype(F32)).astype(BF16)
        for o in (2, 1, 3):
            send(j, "a1", o - 1, s1a.at[j, at(lax.rem(qa + o, 4), TB)], r1a.at[j, o - 1], pa(o))
        s1b[j] = (pk[j, :, DA:] + cr[j, :, DA:].astype(F32)).astype(BF16)
        for o in (2, 1, 3):
            send(j, "b1", o - 1, s1b.at[j, at(lax.rem(qb + o, 4), TB)], r1b.at[j, o - 1], pb(o))

    def stage_2(j):
        (pa, qa), (pb, qb) = axes(j)
        for name, r1, q, k2, s2, r2, lanes, p, me, out in (
                ("a1", r1a, qa, k2a, s2a, r2a, slice(0, DA), pb, qb, "a2"),
                ("b1", r1b, qb, k2b, s2b, r2b, slice(DA, D), pa, qa, "b2")):
            total = pk[j, at(q, TB), lanes] + cr[j, at(q, TB), lanes].astype(F32)
            for i in (0, 2, 1):
                arrive(j, name, i, r1.at[j, i])
                total = total + r1[j, i].astype(F32)
            k2[j] = total
            s2[j] = total.astype(BF16)
            for o in (2, 1, 3):
                send(j, out, o - 1, s2.at[j, at(lax.rem(me + o, 4), PR)], r2.at[j, o - 1], p(o))

    def stage_3(j):
        if j == 0:
            loads[3].wait()
        (pa, qa), (pb, qb) = axes(j)
        for name, r2, me, k2, lanes, q in (("a2", r2a, qb, k2a, slice(0, DA), qa),
                                           ("b2", r2b, qa, k2b, slice(DA, D), qb)):
            total = k2[j, at(me, PR)]
            for i in (0, 2, 1):
                arrive(j, name, i, r2.at[j, i])
                total = total + r2[j, i].astype(F32)
            owner = (q == x).astype(F32)
            total = total - owner * hid[c, pl.ds(pl.multiple_of(j * TB + me * PR, PR), PR), lanes].astype(F32)
            k3[j, :, lanes] = total
            s3[j, :, lanes] = total.astype(BF16)
        for o in (2, 1, 3):
            send(j, "x", o - 1, s3.at[j], r3.at[j, o - 1], xpeer(o))

    def stage_4(j):
        total = k3[j]
        for i in (0, 2, 1):
            arrive(j, "x", i, r3.at[j, i])
            total = total + r3[j, i].astype(F32)
        scaled = (total * inverse).astype(BF16)
        (pa, qa), (pb, qb) = axes(j)
        arows = pl.ds(pl.multiple_of(qa * TB + qb * PR, PR), PR)
        brows = pl.ds(pl.multiple_of(qb * TB + qa * PR, PR), PR)
        sa[c, j, arows] = scaled[:, :DA]
        sb[c, j, brows] = scaled[:, DA:]
        for o in (2, 1, 3):
            send(j, "ga1", o - 1, sa.at[c, j, arows], sa.at[c, j, arows], pb(o))
            send(j, "gb1", o - 1, sb.at[c, j, brows], sb.at[c, j, brows], pa(o))

    def stage_5(j):
        (pa, qa), (pb, qb) = axes(j)
        for i, o in ((0, 3), (2, 1), (1, 2)):
            ra, rb = lax.rem(qa + o, 4), lax.rem(qb + o, 4)
            arrive(j, "ga1", i, sa.at[c, j, pl.ds(pl.multiple_of(qa * TB + rb * PR, PR), PR)])
            arrive(j, "gb1", i, sb.at[c, j, pl.ds(pl.multiple_of(qb * TB + ra * PR, PR), PR)])
        for o in (2, 1, 3):
            send(j, "ga2", o - 1, sa.at[c, j, at(qa, TB)], sa.at[c, j, at(qa, TB)], pa(o))
            send(j, "gb2", o - 1, sb.at[c, j, at(qb, TB)], sb.at[c, j, at(qb, TB)], pb(o))

    def stage_6(j):
        (pa, qa), (pb, qb) = axes(j)
        for i, o in ((0, 3), (2, 1), (1, 2)):
            arrive(j, "ga2", i, sa.at[c, j, at(lax.rem(qa + o, 4), TB)])
            arrive(j, "gb2", i, sb.at[c, j, at(lax.rem(qb + o, 4), TB)])
        send(j, "fa", 0, sa.at[c, j], sa.at[c, j], partner)
        send(j, "fb", 0, sb.at[c, j], sb.at[c, j], partner)

    def stage_7(j):
        arrive(j, "fa", 0, sa.at[other, j])
        arrive(j, "fb", 0, sb.at[other, j])

        total = jnp.zeros((M, Fw), F32)
        for t in range(2):
            part = lax.dot_general(sa[t, j], wo[t, :, :DA], NT, preferred_element_type=F32)
            part = part + lax.dot_general(sb[t, j], wo[t, :, DA:], NT, preferred_element_type=F32)
            total = total + live_of(t) * part
        for t in range(4):
            rows = slice(t * TB, (t + 1) * TB)
            pre = total[rows] * gate[t, j * TB:(j + 1) * TB].astype(F32)
            bias_ref[...] += jnp.sum(pre, axis=0, keepdims=True)
            low[j, rows] = pre.astype(BF16)

    gather_own(0)
    if R > 1:
        gather_own(1)
    stages = {"F": stage_f, "E": stage_e, "1": stage_1, "2": stage_2, "3": stage_3, "4": stage_4, "5": stage_5,
              "6": stage_6, "7": stage_7}
    for item in ORDER:
        stages[item[0]](int(item[1:]))
    for copy in started:
        copy.wait_send()


def grad_kernel(depth_ref, bias_ref, acts, x, low, sa, sb, enc_hbm, dec_hbm, bias_out, enc, dec, out_sem):
    layer = lax.axis_index("layer")
    Fw, D, DA = acts.shape[1], x.shape[1], sa.shape[-1]
    bias_out[...] = bias_ref[...]
    outs = []

    def put(src, dst):
        copy = pltpu.make_async_copy(src, dst, out_sem.at[len(outs)])
        copy.start()
        outs.append(copy)

    for t in range(2):
        live = (layer <= depth_ref[t]).astype(F32)
        for i in range(0, Fw, 512):
            rows = pl.ds(i, 512)
            got = lax.dot_general(acts[:, rows], sa[t], TN, preferred_element_type=F32)
            dec[t, rows, :DA] = (got * live).astype(BF16)
            got = lax.dot_general(acts[:, rows], sb[t], TN, preferred_element_type=F32)
            dec[t, rows, DA:] = (got * live).astype(BF16)
            put(dec.at[t, rows], dec_hbm.at[t, rows])
    for lo, hi in ((0, 512), (512, 896), (896, D)):
        rows = pl.ds(lo, hi - lo)
        got = lax.dot_general(x[:, rows], low[...], TN, preferred_element_type=F32)
        enc[rows] = got.astype(BF16)
        put(enc.at[rows], enc_hbm.at[rows])
    for copy in outs:
        copy.wait()


def step(entries, readin, offset, cutoff, writeout, hidden, depths):
    R = ROUNDS
    tokens, D = entries.shape[1] * 4, entries.shape[2]
    Fw = readin.shape[2]
    TB = tokens // 4 // R
    M, PR, DA = 4 * TB, TB // 4, 640
    DB = D - DA
    cfg = (R, TB, D, DA, Fw, 1.0 / math.sqrt(tokens))
    n_slots = len(sent(R))
    pin = functools.partial(pltpu.with_memory_space_constraint, memory_space=pltpu.HBM)
    hbm = pl.BlockSpec(memory_space=pltpu.HBM)
    vmem = pl.BlockSpec(memory_space=pltpu.VMEM)
    smem = pl.BlockSpec(memory_space=pltpu.SMEM)
    V = pltpu.VMEM
    bias, g, acts, low, sa, sb = pl.pallas_call(
        functools.partial(comm_kernel, cfg),
        out_shape=(
            jax.ShapeDtypeStruct((1, Fw), F32),
            jax.ShapeDtypeStruct((R, M, D), BF16),
            jax.ShapeDtypeStruct((R, M, Fw), BF16),
            jax.ShapeDtypeStruct((R, M, Fw), BF16),
            jax.ShapeDtypeStruct((2, R, M, DA), BF16),
            jax.ShapeDtypeStruct((2, R, M, DB), BF16),
        ),
        in_specs=[smem, hbm, hbm, vmem, hbm, hbm, hbm],
        out_specs=(vmem,) * 6,
        scratch_shapes=[
            V((D, Fw), BF16), V((4, tokens // 4, Fw), jnp.int32), V((2, Fw, D), BF16), V((2, tokens // 4, D), BF16),
            V((R, M, D), F32), V((R, M, D), BF16), V((R, M, D), BF16),
            V((R, M, DA), BF16), V((R, M, DB), BF16), V((R, 3, TB, DA), BF16), V((R, 3, TB, DB), BF16),
            V((R, TB, DA), F32), V((R, TB, DB), F32), V((R, TB, DA), BF16), V((R, TB, DB), BF16),
            V((R, 3, PR, DA), BF16), V((R, 3, PR, DB), BF16),
            V((R, PR, D), F32), V((R, PR, D), BF16), V((R, 3, PR, D), BF16),
            pltpu.SemaphoreType.DMA((R, n_slots)), pltpu.SemaphoreType.DMA((R, n_slots)),
            pltpu.SemaphoreType.DMA((4,)), pltpu.SemaphoreType.DMA((R,)),
        ],
        compiler_params=pltpu.CompilerParams(collective_id=0, has_side_effects=True, vmem_limit_bytes=36 * 2**20),
    )(pin(depths), pin(entries[0]), pin(readin[0]), pin(offset), pin(cutoff.reshape(4, tokens // 4, Fw)), pin(writeout[0]), pin(hidden))

    acts2, low2, g2 = acts.reshape(tokens, Fw), low.reshape(tokens, Fw), g.reshape(tokens, D)
    sa2, sb2 = sa.reshape(2, tokens, DA), sb.reshape(2, tokens, DB)
    enc, dec, bias = pl.pallas_call(
        grad_kernel,
        out_shape=(
            jax.ShapeDtypeStruct((D, Fw), BF16),
            jax.ShapeDtypeStruct((2, Fw, D), BF16),
            jax.ShapeDtypeStruct((1, Fw), F32),
        ),
        in_specs=[smem, vmem, vmem, vmem, vmem, vmem, vmem],
        out_specs=(hbm, hbm, vmem),
        scratch_shapes=[V((D, Fw), BF16), V((2, Fw, D), BF16), pltpu.SemaphoreType.DMA((7,))],
        compiler_params=pltpu.CompilerParams(vmem_limit_bytes=30 * 2**20),
        cost_estimate=pl.CostEstimate(flops=6 * tokens * Fw * D, bytes_accessed=18 * 2**20, transcendentals=0),
    )(pin(depths), bias, acts2, g2, low2, sa2, sb2)
    return enc[None], dec[None], bias


def solution(mesh):
    return jax.shard_map(
        step,
        mesh=mesh,
        in_specs=(
            P("layer", "tok", None),
            P("layer", None, ("feat", "tok")),
            P("layer", ("feat", "tok")),
            P("layer", None, ("feat", "tok")),
            P("layer", None, ("feat", "tok"), None),
            P(None, "tok", None),
            P(),
        ),
        out_specs=(
            P("layer", None, ("feat", "tok")),
            P("layer", None, ("feat", "tok"), None),
            P("layer", ("feat", "tok")),
        ),
        check_vma=False,
    )
```

```python
import functools
import math

import jax
import jax.numpy as jnp
from jax import lax
from jax.experimental import pallas as pl
from jax.experimental.pallas import tpu as pltpu
from jax.sharding import PartitionSpec as P

MESH = pl.DeviceIdType.MESH
F32, BF16 = jnp.float32, jnp.bfloat16
ROUNDS = 4
EARLY = 2
NT = (((1,), (1,)), ((), ()))
TN = (((0,), (0,)), ((), ()))
ORDER = (
    "F0", "F1", "E0", "F2", "10", "E1", "F3", "11", "E2", "20", "E3", "12", "21", "13", "30", "40", "22", "31",
    "23", "50", "32", "41", "33", "42", "60", "51", "43", "70", "52", "a0", "b0", "c0", "61", "53", "71", "62",
    "a1", "b1", "72", "63", "c1", "73",
)


def sent(R):
    slots = {}
    for name, count in (("g", 4), ("p", 1), ("a1", 3), ("b1", 3), ("a2", 3), ("b2", 3), ("x", 3),
                        ("ga1", 3), ("gb1", 3), ("ga2", 3), ("gb2", 3), ("fa", 1), ("fb", 1)):
        for i in range(count):
            slots[name, i] = len(slots)
    return slots


def comm_kernel(cfg, depth_ref, x_hbm, wr_hbm, off_ref, gate_hbm, wo_hbm, hid_hbm,
                bias_ref, g, acts, low, sa, sb, accd, acce,
                wr, gate, wo, hid, cs, cr, s1a, s1b, r1a, r1b, k2a, k2b, s2a, s2b, r2a, r2b,
                k3, s3, r3, send_sem, recv_sem, in_sem, own_sem):
    R, TB, D, DA, Fw, inverse = cfg
    DB = D - DA
    M, PR, HB = 4 * TB, TB // 4, TB // 2
    slots = sent(R)
    layer, feat, x = lax.axis_index("layer"), lax.axis_index("feat"), lax.axis_index("tok")
    c = lax.rem(layer, 2)
    z = lax.rem(lax.div(layer, 2), 4)
    y = lax.div(layer, 8) * 2 + feat
    other = 1 - c

    def live_of(t):
        return (layer <= depth_ref[t]).astype(F32)

    def xpeer(o):
        return (layer, feat, lax.rem(x + o, 4))

    def zpeer(o):
        return (lax.div(layer, 8) * 8 + lax.rem(z + o, 4) * 2 + c, feat, x)

    def ypeer(o):
        yy = lax.rem(y + o, 4)
        return (lax.div(yy, 2) * 8 + z * 2 + c, lax.rem(yy, 2), x)

    def axes(j):
        pairs = ((zpeer, z), (ypeer, y))
        return pairs if j % 2 == 0 else pairs[::-1]

    partner = (lax.div(layer, 2) * 2 + other, feat, x)

    def at(index, size):
        return pl.ds(pl.multiple_of(index * size, size), size)

    def mine(j):
        return pl.ds(j * M, M)

    def remote(j, name, i, src, dst, device):
        k = slots[name, i]
        return pltpu.make_async_remote_copy(
            src_ref=src, dst_ref=dst, send_sem=send_sem.at[j, k], recv_sem=recv_sem.at[j, k],
            device_id=device, device_id_type=MESH)

    started = []

    def send(j, name, i, src, dst, device):
        copy = remote(j, name, i, src, dst, device)
        copy.start()
        started.append(copy)

    def arrive(j, name, i, dst):
        remote(j, name, i, dst, dst, partner).wait_recv()

    loads = [pltpu.make_async_copy(a, b, in_sem.at[i]) for i, (a, b) in enumerate(
        ((wr_hbm, wr), (gate_hbm, gate), (wo_hbm, wo), (hid_hbm, hid)))]
    own = [pltpu.make_async_copy(x_hbm.at[pl.ds(j * TB, TB)], g.at[j, at(x, TB)], own_sem.at[j]) for j in range(R)]
    for j in range(R):
        own[j].start()
    for copy in loads:
        copy.start()
    bias_ref[...] = jnp.zeros_like(bias_ref)

    barrier = pltpu.get_barrier_semaphore()
    peers = [p(o) for p in (xpeer, ypeer, zpeer) for o in (1, 3, 2)] + [partner]
    for p in peers:
        pl.semaphore_signal(barrier, inc=1, device_id=p, device_id_type=MESH)
    pl.semaphore_wait(barrier, len(peers))

    def gather_own(j):
        src = x_hbm.at[pl.ds(j * TB, TB)]
        send(j, "g", 0, src, g.at[j, at(x, TB)], xpeer(1))
        send(j, "g", 1, src, g.at[j, at(x, TB)], xpeer(3))

    def stage_f(j):
        left, right = lax.rem(x + 3, 4), lax.rem(x + 1, 4)
        arrive(j, "g", 0, g.at[j, at(left, TB)])
        rows = pl.ds(pl.multiple_of(left * TB, TB), HB)
        send(j, "g", 2, g.at[j, rows], g.at[j, rows], xpeer(1))
        arrive(j, "g", 1, g.at[j, at(right, TB)])
        rows = pl.ds(pl.multiple_of(right * TB + HB, HB), HB)
        send(j, "g", 3, g.at[j, rows], g.at[j, rows], xpeer(3))
        if j + 2 < R:
            gather_own(j + 2)

    def stage_e(j):
        far = lax.rem(x + 2, 4)
        arrive(j, "g", 2, g.at[j, pl.ds(pl.multiple_of(far * TB, TB), HB)])
        arrive(j, "g", 3, g.at[j, pl.ds(pl.multiple_of(far * TB + HB, HB), HB)])
        own[j].wait()
        if j == 0:
            loads[0].wait()
            loads[1].wait()

        pre = jnp.dot(g[j], wr[...], preferred_element_type=F32) + off_ref[...]
        for t in range(4):
            rows = slice(t * TB, (t + 1) * TB)
            acts[j, rows] = (pre[rows] * gate[t, j * TB:(j + 1) * TB].astype(F32)).astype(BF16)
        if j == 0:
            loads[2].wait()
        part = jnp.dot(acts[j], wo[other], preferred_element_type=F32)
        cs[j] = (part * live_of(other)).astype(BF16)
        send(j, "p", 0, cs.at[j], cr.at[j], partner)
        accd[1, mine(j)] = jnp.dot(acts[j], wo[c], preferred_element_type=F32) * live_of(c)

    def stage_1(j):
        arrive(j, "p", 0, cr.at[j])
        (pa, qa), (pb, qb) = axes(j)
        s1a[j] = (accd[1, mine(j), :DA] + cr[j, :, :DA].astype(F32)).astype(BF16)
        for o in (2, 1, 3):
            send(j, "a1", o - 1, s1a.at[j, at(lax.rem(qa + o, 4), TB)], r1a.at[j, o - 1], pa(o))
        s1b[j] = (accd[1, mine(j), DA:] + cr[j, :, DA:].astype(F32)).astype(BF16)
        for o in (2, 1, 3):
            send(j, "b1", o - 1, s1b.at[j, at(lax.rem(qb + o, 4), TB)], r1b.at[j, o - 1], pb(o))

    def stage_2(j):
        (pa, qa), (pb, qb) = axes(j)
        for name, r1, q, k2, s2, r2, lanes, p, me, out in (
                ("a1", r1a, qa, k2a, s2a, r2a, slice(0, DA), pb, qb, "a2"),
                ("b1", r1b, qb, k2b, s2b, r2b, slice(DA, D), pa, qa, "b2")):
            total = accd[1, pl.ds(pl.multiple_of(j * M + q * TB, TB), TB), lanes] + cr[j, at(q, TB), lanes].astype(F32)
            for i in (0, 2, 1):
                arrive(j, name, i, r1.at[j, i])
                total = total + r1[j, i].astype(F32)
            k2[j] = total
            s2[j] = total.astype(BF16)
            for o in (2, 1, 3):
                send(j, out, o - 1, s2.at[j, at(lax.rem(me + o, 4), PR)], r2.at[j, o - 1], p(o))

    def stage_3(j):
        if j == 0:
            loads[3].wait()
        (pa, qa), (pb, qb) = axes(j)
        for name, r2, me, k2, lanes, q in (("a2", r2a, qb, k2a, slice(0, DA), qa),
                                           ("b2", r2b, qa, k2b, slice(DA, D), qb)):
            total = k2[j, at(me, PR)]
            for i in (0, 2, 1):
                arrive(j, name, i, r2.at[j, i])
                total = total + r2[j, i].astype(F32)
            owner = (q == x).astype(F32)
            total = total - owner * hid[c, pl.ds(pl.multiple_of(j * TB + me * PR, PR), PR), lanes].astype(F32)
            k3[j, :, lanes] = total
            s3[j, :, lanes] = total.astype(BF16)
        for o in (2, 1, 3):
            send(j, "x", o - 1, s3.at[j], r3.at[j, o - 1], xpeer(o))

    def stage_4(j):
        total = k3[j]
        for i in (0, 2, 1):
            arrive(j, "x", i, r3.at[j, i])
            total = total + r3[j, i].astype(F32)
        scaled = (total * inverse).astype(BF16)
        (pa, qa), (pb, qb) = axes(j)
        arows = pl.ds(pl.multiple_of(qa * TB + qb * PR, PR), PR)
        brows = pl.ds(pl.multiple_of(qb * TB + qa * PR, PR), PR)
        sa[c, j, arows] = scaled[:, :DA]
        sb[c, j, brows] = scaled[:, DA:]
        for o in (2, 1, 3):
            send(j, "ga1", o - 1, sa.at[c, j, arows], sa.at[c, j, arows], pb(o))
            send(j, "gb1", o - 1, sb.at[c, j, brows], sb.at[c, j, brows], pa(o))

    def stage_5(j):
        (pa, qa), (pb, qb) = axes(j)
        for i, o in ((0, 3), (2, 1), (1, 2)):
            ra, rb = lax.rem(qa + o, 4), lax.rem(qb + o, 4)
            arrive(j, "ga1", i, sa.at[c, j, pl.ds(pl.multiple_of(qa * TB + rb * PR, PR), PR)])
            arrive(j, "gb1", i, sb.at[c, j, pl.ds(pl.multiple_of(qb * TB + ra * PR, PR), PR)])
        for o in (2, 1, 3):
            send(j, "ga2", o - 1, sa.at[c, j, at(qa, TB)], sa.at[c, j, at(qa, TB)], pa(o))
            send(j, "gb2", o - 1, sb.at[c, j, at(qb, TB)], sb.at[c, j, at(qb, TB)], pb(o))

    def stage_6(j):
        (pa, qa), (pb, qb) = axes(j)
        for i, o in ((0, 3), (2, 1), (1, 2)):
            arrive(j, "ga2", i, sa.at[c, j, at(lax.rem(qa + o, 4), TB)])
            arrive(j, "gb2", i, sb.at[c, j, at(lax.rem(qb + o, 4), TB)])
        send(j, "fa", 0, sa.at[c, j], sa.at[c, j], partner)
        send(j, "fb", 0, sb.at[c, j], sb.at[c, j], partner)

    def stage_7(j):
        arrive(j, "fa", 0, sa.at[other, j])
        arrive(j, "fb", 0, sb.at[other, j])

        total = jnp.zeros((M, Fw), F32)
        for t in range(2):
            part = lax.dot_general(sa[t, j], wo[t, :, :DA], NT, preferred_element_type=F32)
            part = part + lax.dot_general(sb[t, j], wo[t, :, DA:], NT, preferred_element_type=F32)
            total = total + live_of(t) * part
        for t in range(4):
            rows = slice(t * TB, (t + 1) * TB)
            pre = total[rows] * gate[t, j * TB:(j + 1) * TB].astype(F32)
            bias_ref[...] += jnp.sum(pre, axis=0, keepdims=True)
            low[j, rows] = pre.astype(BF16)

    def grad(t, j):
        for i in range(0, Fw, 512):
            rows = pl.ds(i, 512)
            for ref, lanes in ((sa, slice(0, DA)), (sb, slice(DA, D))):
                got = lax.dot_general(acts[j, :, rows], ref[t, j], TN, preferred_element_type=F32)
                accd[t, rows, lanes] = got if j == 0 else accd[t, rows, lanes] + got

    def stage_c(j):
        for lo, hi in ((0, 512), (512, 896), (896, D)):
            rows = pl.ds(lo, hi - lo)
            got = lax.dot_general(g[j, :, rows], low[j], TN, preferred_element_type=F32)
            acce[rows] = got if j == 0 else acce[rows] + got

    gather_own(0)
    if R > 1:
        gather_own(1)
    stages = {"F": stage_f, "E": stage_e, "1": stage_1, "2": stage_2, "3": stage_3, "4": stage_4, "5": stage_5,
              "6": stage_6, "7": stage_7, "a": functools.partial(grad, 0), "b": functools.partial(grad, 1), "c": stage_c}
    for item in ORDER:
        stages[item[0]](int(item[1:]))
    for copy in started:
        copy.wait_send()


def grad_kernel(skip, depth_ref, bias_ref, acts, x, low, sa, sb, accd, acce, enc_hbm, dec_hbm, bias_out, enc, dec, out_sem):
    layer = lax.axis_index("layer")
    Fw, D, DA = acts.shape[1], x.shape[1], sa.shape[-1]
    bias_out[...] = bias_ref[...]
    outs = []

    def put(src, dst):
        copy = pltpu.make_async_copy(src, dst, out_sem.at[len(outs)])
        copy.start()
        outs.append(copy)

    late = slice(skip, acts.shape[0])
    for t in range(2):
        live = (layer <= depth_ref[t]).astype(F32)
        for i in range(0, Fw, 512):
            rows = pl.ds(i, 512)
            for ref, lanes in ((sa, slice(0, DA)), (sb, slice(DA, D))):
                got = lax.dot_general(acts[late, rows], ref[t, late], TN, preferred_element_type=F32)
                dec[t, rows, lanes] = ((accd[t, rows, lanes] + got) * live).astype(BF16)
            put(dec.at[t, rows], dec_hbm.at[t, rows])
    for lo, hi in ((0, 512), (512, 896), (896, D)):
        rows = pl.ds(lo, hi - lo)
        got = lax.dot_general(x[late, rows], low[late], TN, preferred_element_type=F32)
        enc[rows] = (acce[rows] + got).astype(BF16)
        put(enc.at[rows], enc_hbm.at[rows])
    for copy in outs:
        copy.wait()


def step(entries, readin, offset, cutoff, writeout, hidden, depths):
    R = ROUNDS
    tokens, D = entries.shape[1] * 4, entries.shape[2]
    Fw = readin.shape[2]
    TB = tokens // 4 // R
    M, PR, DA = 4 * TB, TB // 4, 640
    DB = D - DA
    cfg = (R, TB, D, DA, Fw, 1.0 / math.sqrt(tokens))
    n_slots = len(sent(R))
    pin = functools.partial(pltpu.with_memory_space_constraint, memory_space=pltpu.HBM)
    hbm = pl.BlockSpec(memory_space=pltpu.HBM)
    vmem = pl.BlockSpec(memory_space=pltpu.VMEM)
    smem = pl.BlockSpec(memory_space=pltpu.SMEM)
    V = pltpu.VMEM
    bias, g, acts, low, sa, sb, accd, acce = pl.pallas_call(
        functools.partial(comm_kernel, cfg),
        out_shape=(
            jax.ShapeDtypeStruct((1, Fw), F32),
            jax.ShapeDtypeStruct((R, M, D), BF16),
            jax.ShapeDtypeStruct((R, M, Fw), BF16),
            jax.ShapeDtypeStruct((R, M, Fw), BF16),
            jax.ShapeDtypeStruct((2, R, M, DA), BF16),
            jax.ShapeDtypeStruct((2, R, M, DB), BF16),
            jax.ShapeDtypeStruct((2, Fw, D), F32),
            jax.ShapeDtypeStruct((D, Fw), F32),
        ),
        in_specs=[smem, hbm, hbm, vmem, hbm, hbm, hbm],
        out_specs=(vmem,) * 8,
        scratch_shapes=[
            V((D, Fw), BF16), V((4, tokens // 4, Fw), jnp.int32), V((2, Fw, D), BF16), V((2, tokens // 4, D), BF16),
            V((R, M, D), BF16), V((R, M, D), BF16),
            V((R, M, DA), BF16), V((R, M, DB), BF16), V((R, 3, TB, DA), BF16), V((R, 3, TB, DB), BF16),
            V((R, TB, DA), F32), V((R, TB, DB), F32), V((R, TB, DA), BF16), V((R, TB, DB), BF16),
            V((R, 3, PR, DA), BF16), V((R, 3, PR, DB), BF16),
            V((R, PR, D), F32), V((R, PR, D), BF16), V((R, 3, PR, D), BF16),
            pltpu.SemaphoreType.DMA((R, n_slots)), pltpu.SemaphoreType.DMA((R, n_slots)),
            pltpu.SemaphoreType.DMA((4,)), pltpu.SemaphoreType.DMA((R,)),
        ],
        compiler_params=pltpu.CompilerParams(collective_id=0, has_side_effects=True, vmem_limit_bytes=27 * 2**20),
    )(pin(depths), pin(entries[0]), pin(readin[0]), pin(offset), pin(cutoff.reshape(4, tokens // 4, Fw)), pin(writeout[0]), pin(hidden))

    acts2, low2, g2 = acts.reshape(tokens, Fw), low.reshape(tokens, Fw), g.reshape(tokens, D)
    sa2, sb2 = sa.reshape(2, tokens, DA), sb.reshape(2, tokens, DB)
    enc, dec, bias = pl.pallas_call(
        functools.partial(grad_kernel, EARLY * M),
        out_shape=(
            jax.ShapeDtypeStruct((D, Fw), BF16),
            jax.ShapeDtypeStruct((2, Fw, D), BF16),
            jax.ShapeDtypeStruct((1, Fw), F32),
        ),
        in_specs=[smem] + [vmem] * 8,
        out_specs=(hbm, hbm, vmem),
        scratch_shapes=[V((D, Fw), BF16), V((2, Fw, D), BF16), pltpu.SemaphoreType.DMA((7,))],
        compiler_params=pltpu.CompilerParams(vmem_limit_bytes=14 * 2**20),
        cost_estimate=pl.CostEstimate(flops=6 * tokens * Fw * D, bytes_accessed=18 * 2**20, transcendentals=0),
    )(pin(depths), bias, acts2, g2, low2, sa2, sb2, accd, acce)
    return enc[None], dec[None], bias


def solution(mesh):
    return jax.shard_map(
        step,
        mesh=mesh,
        in_specs=(
            P("layer", "tok", None),
            P("layer", None, ("feat", "tok")),
            P("layer", ("feat", "tok")),
            P("layer", None, ("feat", "tok")),
            P("layer", None, ("feat", "tok"), None),
            P(None, "tok", None),
            P(),
        ),
        out_specs=(
            P("layer", None, ("feat", "tok")),
            P("layer", None, ("feat", "tok"), None),
            P("layer", ("feat", "tok")),
        ),
        check_vma=False,
    )
```

```python
import functools
import math

import jax
import jax.numpy as jnp
from jax import lax
from jax.experimental import pallas as pl
from jax.experimental.pallas import tpu as pltpu
from jax.sharding import PartitionSpec as P

MESH = pl.DeviceIdType.MESH
F32, BF16 = jnp.float32, jnp.bfloat16
ROUNDS = 4
EARLY = 2
NT = (((1,), (1,)), ((), ()))
TN = (((0,), (0,)), ((), ()))
ORDER = (
    "F0", "F1", "E0", "F2", "10", "E1", "F3", "11", "E2", "20", "12", "E3", "13", "21", "30", "22", "40", "23",
    "31", "32", "50", "33", "41", "42", "43", "60", "51", "52", "70", "a0", "53", "b0", "c0", "61", "71", "62",
    "a1", "b1", "72", "63", "c1", "73",
)


def sent(R):
    slots = {}
    for name, count in (("g", 4), ("p", 1), ("a1", 3), ("b1", 3), ("a2", 3), ("b2", 3), ("x", 3),
                        ("ga1", 3), ("gb1", 3), ("ga2", 3), ("gb2", 3), ("fa", 1), ("fb", 1)):
        for i in range(count):
            slots[name, i] = len(slots)
    return slots


def comm_kernel(cfg, depth_ref, x_hbm, wr_hbm, off_ref, gate_hbm, wo_hbm, hid_hbm,
                bias_ref, g, acts, low, sa, sb, accd, acce,
                wr, gate, wo, hid, cs, cr, s1a, s1b, r1a, r1b, k2a, k2b, s2a, s2b, r2a, r2b,
                k3, s3, r3, half, send_sem, recv_sem, in_sem, own_sem):
    R, TB, D, DA, Fw, inverse = cfg
    DB = D - DA
    M, PR, HB = 4 * TB, TB // 4, TB // 2
    slots = sent(R)
    layer, feat, x = lax.axis_index("layer"), lax.axis_index("feat"), lax.axis_index("tok")
    c = lax.rem(layer, 2)
    z = lax.rem(lax.div(layer, 2), 4)
    y = lax.div(layer, 8) * 2 + feat
    other = 1 - c

    def live_of(t):
        return (layer <= depth_ref[t]).astype(F32)

    def xpeer(o):
        return (layer, feat, lax.rem(x + o, 4))

    def zpeer(o):
        return (lax.div(layer, 8) * 8 + lax.rem(z + o, 4) * 2 + c, feat, x)

    def ypeer(o):
        yy = lax.rem(y + o, 4)
        return (lax.div(yy, 2) * 8 + z * 2 + c, lax.rem(yy, 2), x)

    def axes(j):
        pairs = ((zpeer, z), (ypeer, y))
        return pairs if j % 2 == 0 else pairs[::-1]

    partner = (lax.div(layer, 2) * 2 + other, feat, x)

    def at(index, size):
        return pl.ds(pl.multiple_of(index * size, size), size)

    def mine(j):
        return pl.ds(j * M, M)

    def remote(j, name, i, src, dst, device):
        k = slots[name, i]
        return pltpu.make_async_remote_copy(
            src_ref=src, dst_ref=dst, send_sem=send_sem.at[j, k], recv_sem=recv_sem.at[j, k],
            device_id=device, device_id_type=MESH)

    started = []

    def send(j, name, i, src, dst, device):
        copy = remote(j, name, i, src, dst, device)
        copy.start()
        started.append(copy)

    def arrive(j, name, i, dst):
        remote(j, name, i, dst, dst, partner).wait_recv()

    loads = [pltpu.make_async_copy(a, b, in_sem.at[i]) for i, (a, b) in enumerate(
        ((wr_hbm, wr), (gate_hbm, gate), (wo_hbm, wo), (hid_hbm, hid)))]
    own = [pltpu.make_async_copy(x_hbm.at[pl.ds(j * TB, TB)], g.at[j, at(x, TB)], own_sem.at[j]) for j in range(R)]
    for j in range(R):
        own[j].start()
    for copy in loads:
        copy.start()
    bias_ref[...] = jnp.zeros_like(bias_ref)

    barrier = pltpu.get_barrier_semaphore()
    peers = [p(o) for p in (xpeer, ypeer, zpeer) for o in (1, 3, 2)] + [partner]
    for p in peers:
        pl.semaphore_signal(barrier, inc=1, device_id=p, device_id_type=MESH)
    pl.semaphore_wait(barrier, len(peers))

    def gather_own(j):
        src = x_hbm.at[pl.ds(j * TB, TB)]
        send(j, "g", 0, src, g.at[j, at(x, TB)], xpeer(1))
        send(j, "g", 1, src, g.at[j, at(x, TB)], xpeer(3))

    def stage_f(j):
        left, right = lax.rem(x + 3, 4), lax.rem(x + 1, 4)
        arrive(j, "g", 0, g.at[j, at(left, TB)])
        rows = pl.ds(pl.multiple_of(left * TB, TB), HB)
        send(j, "g", 2, g.at[j, rows], g.at[j, rows], xpeer(1))
        arrive(j, "g", 1, g.at[j, at(right, TB)])
        rows = pl.ds(pl.multiple_of(right * TB + HB, HB), HB)
        send(j, "g", 3, g.at[j, rows], g.at[j, rows], xpeer(3))
        if j + 2 < R:
            gather_own(j + 2)

    def stage_e(j):
        far = lax.rem(x + 2, 4)
        arrive(j, "g", 2, g.at[j, pl.ds(pl.multiple_of(far * TB, TB), HB)])
        arrive(j, "g", 3, g.at[j, pl.ds(pl.multiple_of(far * TB + HB, HB), HB)])
        own[j].wait()
        if j == 0:
            loads[0].wait()
            loads[1].wait()

        pre = jnp.dot(g[j], wr[...], preferred_element_type=F32) + off_ref[...]
        for t in range(4):
            rows = slice(t * TB, (t + 1) * TB)
            acts[j, rows] = (pre[rows] * gate[t, j * TB:(j + 1) * TB].astype(F32)).astype(BF16)
        if j == 0:
            loads[2].wait()
        part = jnp.dot(acts[j], wo[other], preferred_element_type=F32)
        cs[j] = (part * live_of(other)).astype(BF16)
        send(j, "p", 0, cs.at[j], cr.at[j], partner)
        accd[1, mine(j)] = jnp.dot(acts[j], wo[c], preferred_element_type=F32) * live_of(c)

    def stage_1(j):
        arrive(j, "p", 0, cr.at[j])
        (pa, qa), (pb, qb) = axes(j)
        s1a[j] = (accd[1, mine(j), :DA] + cr[j, :, :DA].astype(F32)).astype(BF16)
        for o in (2, 1, 3):
            send(j, "a1", o - 1, s1a.at[j, at(lax.rem(qa + o, 4), TB)], r1a.at[j, o - 1], pa(o))
        s1b[j] = (accd[1, mine(j), DA:] + cr[j, :, DA:].astype(F32)).astype(BF16)
        for o in (2, 1, 3):
            send(j, "b1", o - 1, s1b.at[j, at(lax.rem(qb + o, 4), TB)], r1b.at[j, o - 1], pb(o))

    def stage_2(j):
        (pa, qa), (pb, qb) = axes(j)
        for name, r1, q, k2, s2, r2, lanes, p, me, out in (
                ("a1", r1a, qa, k2a, s2a, r2a, slice(0, DA), pb, qb, "a2"),
                ("b1", r1b, qb, k2b, s2b, r2b, slice(DA, D), pa, qa, "b2")):
            total = accd[1, pl.ds(pl.multiple_of(j * M + q * TB, TB), TB), lanes] + cr[j, at(q, TB), lanes].astype(F32)
            for i in (0, 2, 1):
                arrive(j, name, i, r1.at[j, i])
                total = total + r1[j, i].astype(F32)
            k2[j] = total
            s2[j] = total.astype(BF16)
            for o in (2, 1, 3):
                send(j, out, o - 1, s2.at[j, at(lax.rem(me + o, 4), PR)], r2.at[j, o - 1], p(o))

    def stage_3(j):
        if j == 0:
            loads[3].wait()
        (pa, qa), (pb, qb) = axes(j)
        for name, r2, me, k2, lanes, q in (("a2", r2a, qb, k2a, slice(0, DA), qa),
                                           ("b2", r2b, qa, k2b, slice(DA, D), qb)):
            total = k2[j, at(me, PR)]
            for i in (0, 2, 1):
                arrive(j, name, i, r2.at[j, i])
                total = total + r2[j, i].astype(F32)
            owner = (q == x).astype(F32)
            total = total - owner * hid[c, pl.ds(pl.multiple_of(j * TB + me * PR, PR), PR), lanes].astype(F32)
            k3[j, :, lanes] = total
            s3[j, :, lanes] = total.astype(BF16)
        for o in (2, 1, 3):
            send(j, "x", o - 1, s3.at[j], r3.at[j, o - 1], xpeer(o))

    def stage_4(j):
        total = k3[j]
        for i in (0, 2, 1):
            arrive(j, "x", i, r3.at[j, i])
            total = total + r3[j, i].astype(F32)
        scaled = (total * inverse).astype(BF16)
        (pa, qa), (pb, qb) = axes(j)
        arows = pl.ds(pl.multiple_of(qa * TB + qb * PR, PR), PR)
        brows = pl.ds(pl.multiple_of(qb * TB + qa * PR, PR), PR)
        sa[c, j, arows] = scaled[:, :DA]
        sb[c, j, brows] = scaled[:, DA:]
        for o in (2, 1, 3):
            send(j, "ga1", o - 1, sa.at[c, j, arows], sa.at[c, j, arows], pb(o))
            send(j, "gb1", o - 1, sb.at[c, j, brows], sb.at[c, j, brows], pa(o))

    def stage_5(j):
        (pa, qa), (pb, qb) = axes(j)
        for i, o in ((0, 3), (2, 1), (1, 2)):
            ra, rb = lax.rem(qa + o, 4), lax.rem(qb + o, 4)
            arrive(j, "ga1", i, sa.at[c, j, pl.ds(pl.multiple_of(qa * TB + rb * PR, PR), PR)])
            arrive(j, "gb1", i, sb.at[c, j, pl.ds(pl.multiple_of(qb * TB + ra * PR, PR), PR)])
        for o in (2, 1, 3):
            send(j, "ga2", o - 1, sa.at[c, j, at(qa, TB)], sa.at[c, j, at(qa, TB)], pa(o))
            send(j, "gb2", o - 1, sb.at[c, j, at(qb, TB)], sb.at[c, j, at(qb, TB)], pb(o))

    def act_grad(t, j):
        part = lax.dot_general(sa[t, j], wo[t, :, :DA], NT, preferred_element_type=F32)
        part = part + lax.dot_general(sb[t, j], wo[t, :, DA:], NT, preferred_element_type=F32)
        return live_of(t) * part

    def stage_6(j):
        (pa, qa), (pb, qb) = axes(j)
        for i, o in ((0, 3), (2, 1), (1, 2)):
            arrive(j, "ga2", i, sa.at[c, j, at(lax.rem(qa + o, 4), TB)])
            arrive(j, "gb2", i, sb.at[c, j, at(lax.rem(qb + o, 4), TB)])
        send(j, "fa", 0, sa.at[c, j], sa.at[c, j], partner)
        send(j, "fb", 0, sb.at[c, j], sb.at[c, j], partner)

        if j == R - 1:
            half[...] = act_grad(c, j)

    def stage_7(j):
        arrive(j, "fa", 0, sa.at[other, j])
        arrive(j, "fb", 0, sb.at[other, j])

        if j == R - 1:
            total = half[...] + act_grad(other, j)
        else:
            total = act_grad(0, j) + act_grad(1, j)
        for t in range(4):
            rows = slice(t * TB, (t + 1) * TB)
            pre = total[rows] * gate[t, j * TB:(j + 1) * TB].astype(F32)
            bias_ref[...] += jnp.sum(pre, axis=0, keepdims=True)
            low[j, rows] = pre.astype(BF16)

    def grad(t, j):
        for i in range(0, Fw, 512):
            rows = pl.ds(i, 512)
            for ref, lanes in ((sa, slice(0, DA)), (sb, slice(DA, D))):
                got = lax.dot_general(acts[j, :, rows], ref[t, j], TN, preferred_element_type=F32)
                accd[t, rows, lanes] = got if j == 0 else accd[t, rows, lanes] + got

    def stage_c(j):
        for lo, hi in ((0, 512), (512, 896), (896, D)):
            rows = pl.ds(lo, hi - lo)
            got = lax.dot_general(g[j, :, rows], low[j], TN, preferred_element_type=F32)
            acce[rows] = got if j == 0 else acce[rows] + got

    gather_own(0)
    if R > 1:
        gather_own(1)
    stages = {"F": stage_f, "E": stage_e, "1": stage_1, "2": stage_2, "3": stage_3, "4": stage_4, "5": stage_5,
              "6": stage_6, "7": stage_7, "a": functools.partial(grad, 0), "b": functools.partial(grad, 1), "c": stage_c}
    for item in ORDER:
        stages[item[0]](int(item[1:]))
    for copy in started:
        copy.wait_send()


def grad_kernel(skip, depth_ref, bias_ref, acts, x, low, sa, sb, accd, acce, enc_hbm, dec_hbm, bias_out, enc, dec, out_sem):
    layer = lax.axis_index("layer")
    Fw, D, DA = acts.shape[1], x.shape[1], sa.shape[-1]
    bias_out[...] = bias_ref[...]
    outs = []

    def put(src, dst):
        copy = pltpu.make_async_copy(src, dst, out_sem.at[len(outs)])
        copy.start()
        outs.append(copy)

    late = slice(skip, acts.shape[0])
    for t in range(2):
        live = (layer <= depth_ref[t]).astype(F32)
        for i in range(0, Fw, 512):
            rows = pl.ds(i, 512)
            for ref, lanes in ((sa, slice(0, DA)), (sb, slice(DA, D))):
                got = lax.dot_general(acts[late, rows], ref[t, late], TN, preferred_element_type=F32)
                dec[t, rows, lanes] = ((accd[t, rows, lanes] + got) * live).astype(BF16)
            put(dec.at[t, rows], dec_hbm.at[t, rows])
    for lo, hi in ((0, 512), (512, 896), (896, D)):
        rows = pl.ds(lo, hi - lo)
        got = lax.dot_general(x[late, rows], low[late], TN, preferred_element_type=F32)
        enc[rows] = (acce[rows] + got).astype(BF16)
        put(enc.at[rows], enc_hbm.at[rows])
    for copy in outs:
        copy.wait()


def step(entries, readin, offset, cutoff, writeout, hidden, depths):
    R = ROUNDS
    tokens, D = entries.shape[1] * 4, entries.shape[2]
    Fw = readin.shape[2]
    TB = tokens // 4 // R
    M, PR, DA = 4 * TB, TB // 4, 640
    DB = D - DA
    cfg = (R, TB, D, DA, Fw, 1.0 / math.sqrt(tokens))
    n_slots = len(sent(R))
    pin = functools.partial(pltpu.with_memory_space_constraint, memory_space=pltpu.HBM)
    hbm = pl.BlockSpec(memory_space=pltpu.HBM)
    vmem = pl.BlockSpec(memory_space=pltpu.VMEM)
    smem = pl.BlockSpec(memory_space=pltpu.SMEM)
    V = pltpu.VMEM
    bias, g, acts, low, sa, sb, accd, acce = pl.pallas_call(
        functools.partial(comm_kernel, cfg),
        out_shape=(
            jax.ShapeDtypeStruct((1, Fw), F32),
            jax.ShapeDtypeStruct((R, M, D), BF16),
            jax.ShapeDtypeStruct((R, M, Fw), BF16),
            jax.ShapeDtypeStruct((R, M, Fw), BF16),
            jax.ShapeDtypeStruct((2, R, M, DA), BF16),
            jax.ShapeDtypeStruct((2, R, M, DB), BF16),
            jax.ShapeDtypeStruct((2, Fw, D), F32),
            jax.ShapeDtypeStruct((D, Fw), F32),
        ),
        in_specs=[smem, hbm, hbm, vmem, hbm, hbm, hbm],
        out_specs=(vmem,) * 8,
        scratch_shapes=[
            V((D, Fw), BF16), V((4, tokens // 4, Fw), jnp.int32), V((2, Fw, D), BF16), V((2, tokens // 4, D), BF16),
            V((R, M, D), BF16), V((R, M, D), BF16),
            V((R, M, DA), BF16), V((R, M, DB), BF16), V((R, 3, TB, DA), BF16), V((R, 3, TB, DB), BF16),
            V((R, TB, DA), F32), V((R, TB, DB), F32), V((R, TB, DA), BF16), V((R, TB, DB), BF16),
            V((R, 3, PR, DA), BF16), V((R, 3, PR, DB), BF16),
            V((R, PR, D), F32), V((R, PR, D), BF16), V((R, 3, PR, D), BF16), V((M, Fw), F32),
            pltpu.SemaphoreType.DMA((R, n_slots)), pltpu.SemaphoreType.DMA((R, n_slots)),
            pltpu.SemaphoreType.DMA((4,)), pltpu.SemaphoreType.DMA((R,)),
        ],
        compiler_params=pltpu.CompilerParams(collective_id=0, has_side_effects=True, vmem_limit_bytes=27 * 2**20),
    )(pin(depths), pin(entries[0]), pin(readin[0]), pin(offset), pin(cutoff.reshape(4, tokens // 4, Fw)), pin(writeout[0]), pin(hidden))

    acts2, low2, g2 = acts.reshape(tokens, Fw), low.reshape(tokens, Fw), g.reshape(tokens, D)
    sa2, sb2 = sa.reshape(2, tokens, DA), sb.reshape(2, tokens, DB)
    enc, dec, bias = pl.pallas_call(
        functools.partial(grad_kernel, EARLY * M),
        out_shape=(
            jax.ShapeDtypeStruct((D, Fw), BF16),
            jax.ShapeDtypeStruct((2, Fw, D), BF16),
            jax.ShapeDtypeStruct((1, Fw), F32),
        ),
        in_specs=[smem] + [vmem] * 8,
        out_specs=(hbm, hbm, vmem),
        scratch_shapes=[V((D, Fw), BF16), V((2, Fw, D), BF16), pltpu.SemaphoreType.DMA((7,))],
        compiler_params=pltpu.CompilerParams(vmem_limit_bytes=14 * 2**20),
        cost_estimate=pl.CostEstimate(flops=6 * tokens * Fw * D, bytes_accessed=18 * 2**20, transcendentals=0),
    )(pin(depths), bias, acts2, g2, low2, sa2, sb2, accd, acce)
    return enc[None], dec[None], bias


def solution(mesh):
    return jax.shard_map(
        step,
        mesh=mesh,
        in_specs=(
            P("layer", "tok", None),
            P("layer", None, ("feat", "tok")),
            P("layer", ("feat", "tok")),
            P("layer", None, ("feat", "tok")),
            P("layer", None, ("feat", "tok"), None),
            P(None, "tok", None),
            P(),
        ),
        out_specs=(
            P("layer", None, ("feat", "tok")),
            P("layer", None, ("feat", "tok"), None),
            P("layer", ("feat", "tok")),
        ),
        check_vma=False,
    )
```
